32 devices in a mesh: seq: 2 (over y), outer: 4 (over x, core), inner: 4 (over z).
Axes of the slice: x: 2, y: 2, z: 4, core: 2. Of those that a mesh axis runs over, the one named last changes fastest.
Arguments:
- tokens: bfloat16 [4096, 4096], P(('seq', 'outer', 'inner')), parts along dimension 0, may hold values from -6 to 6
- att_ids: int32 [4096, 2, 2], P(('seq', 'outer', 'inner')), parts along dimension 0, may hold values from 0 to 3, all different within a row
- mlp_ids: int32 [4096, 8], P(('seq', 'outer', 'inner')), parts along dimension 0, may hold values from 0 to 31, all different within a row; in each aligned block of 128 rows (0 to 127, 128 to 255, ...) at most 40 rows name the same one
- att_gain: float32 [4096], replicated, may hold values from 0.25 to 1.75
- att_in: bfloat16 [4096, 768], P('inner'), may hold values from -16 to 16
- att_router: bfloat16 [4096, 8], P('inner'), may hold values from -0.09375 to 0.09375
- att_out: bfloat16 [512, 4096], P(None, 'inner'), may hold values from -0.75 to 0.75
- mlp_gain: float32 [4096], replicated, may hold values from 0.25 to 1.75
- mlp_router: bfloat16 [4096, 32], replicated, may hold values from -0.09375 to 0.09375
- w_up: bfloat16 [32, 4096, 256], P(('outer', 'inner')), may hold values from -0.09375 to 0.09375
- w_down: bfloat16 [32, 256, 4096], P(('outer', 'inner')), may hold values from -0.375 to 0.375
Outputs:
- layer_out: bfloat16 [4096, 4096], P(('seq', 'outer', 'inner')), parts along dimension 0
The draws below stay inside these ranges and needn't reach their ends.
There are 2 independent parts, one for each index of `seq`. The reference program is written for one: setup_inputs(seed, part) draws one part's arguments, and reference() takes and returns one part's arrays. A program takes and returns all parts, laid end to end along the dimension named above; an argument that names none is the same for every part. Nothing has to cross between parts.
Inputs may be any that keep to these rules, and one draw needn't show every extreme that they name: `att_ids`: the 2 ids of one token and head differ. `mlp_ids`: among the rows of one device each expert is named at most 40 times, a bound that some block reaches in some devices' rows.
All inputs are finite; a program needn't handle non-finite values.
Results may differ from the reference program's by a relative error of at most 0.008.
Values may be sent and summed in bfloat16 or wider, within the bound.
No kernel may reach another device: no remote copies, remote signals or barrier semaphores. Data moves between devices by JAX's collectives and lax.ppermute only.
A program may use at most 128 MiB of HBM per device.

```python
import math
import jax
import jax.numpy as jnp
import numpy as np
from jax import lax

D = 4096
HEADS = 2
HDIM = 64
ATT_EXP = 4
ATT_TOP = 2
MLP_HID = 256
MLP_TOP = 8
TOK_DEV = 128
EXPERTS = 32
CAP = 40
TOKENS = 2048
N_OUTER = 4
N_INNER = 4


def draw_att_in(key, part):
    columns = 2 * HEADS * HDIM + HEADS * ATT_EXP * HDIM
    weights = jax.random.normal(jax.random.fold_in(key, 11), (D, columns), jnp.float32) * D ** (-0.5)
    return weights.astype(jnp.bfloat16)


def steps_of(own_key, shape, shards, smallest, high):
    loudness = 1.0
    for dim, shards_of in shards:
        draws = jax.random.uniform(jax.random.fold_in(jax.random.fold_in(own_key, 6), dim), (shards_of,), jnp.float32, smallest / len(shards), high / len(shards))
        loudness = loudness * jnp.repeat(jnp.exp(draws), shape[dim] // shards_of).reshape((-1,) + (1,) * (len(shape) - 1 - dim))
    return loudness


def distinct(key, rows, number_of, top, lift):
    ranking = jax.random.permutation(jax.random.fold_in(key, 1), number_of)
    pull = ranking
    for power in range(3):
        pull = pull * pull // number_of
    pull = pull * lift // number_of
    chance = jax.random.randint(jax.random.fold_in(key, 2), (rows, number_of), 0, 4096) + pull
    holders = jax.random.permutation(jax.random.fold_in(key, 3), rows)[jnp.arange(number_of) % rows]
    chance = jnp.where(jnp.arange(rows)[:, None] == holders[None, :], 1 << 14, chance)
    merit = chance * number_of + jnp.arange(number_of)
    return lax.top_k(merit.astype(jnp.int32), top)[1].astype(jnp.int32)


def routed_block(stream_key, own, number, rows, number_of, top, most, skew):
    sequence = jax.random.permutation(stream_key, number_of)
    heavy_load, ordinary = portions_of(number_of, rows * top, most, skew, True), portions_of(number_of, rows * top, most, skew, False)
    places = jnp.arange(number_of)

    def named(lengths, rotation):
        used = int((lengths > 0).sum())
        fixed = max(1, used // 4)
        shifted = fixed + (places - fixed + rotation * (used - fixed)) % max(1, number_of - fixed)
        return jnp.zeros((number_of,), jnp.int32).at[sequence[jnp.where(places < fixed, places, shifted)]].set(jnp.asarray(lengths, jnp.int32))

    lengths = jnp.where(number % 4 == 0, named(heavy_load, number // 4), named(ordinary, number - number // 4 - 1))
    mixed = jax.random.permutation(jax.random.fold_in(own, 3), number_of)
    donor, sink = mixed[0:number_of // 2 * 2:2], mixed[1:number_of // 2 * 2:2]
    room = jnp.minimum(lengths[donor] - 1, most - lengths[sink]) // 2
    room = jnp.where((donor == sequence[0]) | (sink == sequence[0]) | (lengths[sink] == 0), 0, jnp.maximum(room, 0))
    shifted = jax.random.randint(jax.random.fold_in(own, 4), (number_of // 2,), 0, 1 << 20) % (room + 1)
    lengths = lengths.at[donor].add(-shifted).at[sink].add(shifted)
    items = jnp.searchsorted(jnp.cumsum(lengths), jnp.arange(rows * top), side="right").astype(jnp.int32)
    listing = items.reshape(top, rows).T
    listing = listing[jax.random.permutation(jax.random.fold_in(own, 1), rows)]
    rotation = jax.random.randint(jax.random.fold_in(own, 2), (rows, 1), 0, top)
    return jnp.take_along_axis(listing, (jnp.arange(top)[None, :] + rotation) % top, axis=1)


def portions_of(amount, total, reach, skew, full):
    loads = [(1 << 20) // math.isqrt(rank ** skew) + 1 for rank in range(1, amount + 1)]
    largest = reach if full else min(reach, max(-(-total // amount), total * loads[0] // sum(loads)))
    least = 1 if total - largest >= amount - 1 else 0
    given, rest = [largest] + [least] * (amount - 1), total - largest - least * (amount - 1)
    while rest > 0:
        movable = [i for i in range(1, amount) if given[i] < largest] or [i for i in range(1, amount) if given[i] < reach]
        whole, remaining = sum([loads[i] for i in movable]), rest
        for i in movable:
            more = min(reach - given[i], max(1, remaining * loads[i] // whole), rest)
            given[i] = given[i] + more
            rest = rest - more
    return np.array(given)


def scatter_about(rng, shape, scale, bound, pieces=(), kind=jnp.bfloat16):
    entries = jax.random.normal(rng, shape, jnp.float32) * scale
    if len(pieces) > 0:
        entries = steps_of(rng, shape, pieces, -0.22, 0.18) * entries
    return jnp.clip(entries, min=-bound, max=bound).astype(kind)


def setup_inputs(seed: int = 0, part: int = 0) -> dict:
    streams_of = jax.random.split(jax.random.key(seed), 12)
    part_keys = jax.random.split(jax.random.fold_in(streams_of[11], part), 12)
    tokens = scatter_about(part_keys[0], (TOKENS, D), 1.0, 6.0, ((0, 16),))
    att_ids = distinct(part_keys[1], TOKENS * HEADS, ATT_EXP, ATT_TOP, 4096).reshape((TOKENS, HEADS, ATT_TOP))
    mlp_ids_keys = jax.random.split(jax.random.fold_in(part_keys[2], 1), TOKENS // TOK_DEV)
    mlp_ids_turns = jax.random.permutation(jax.random.fold_in(part_keys[2], 3), TOKENS // TOK_DEV)
    mlp_ids = jax.vmap(lambda own, number: routed_block(jax.random.fold_in(part_keys[2], 2), own, number, TOK_DEV, EXPERTS, MLP_TOP, CAP, 2))(mlp_ids_keys, mlp_ids_turns).reshape((TOKENS, MLP_TOP))
    att_gain = jnp.clip(1.0 + 0.15 * jax.random.normal(streams_of[3], (D,), jnp.float32), 0.25, 1.75)
    att_in = draw_att_in(jax.random.fold_in(streams_of[11], 71), part)
    att_router = scatter_about(streams_of[5], (D, HEADS * ATT_EXP), D ** -0.5, 0.09375, ((0, 4),))
    att_out = scatter_about(streams_of[6], (HEADS * ATT_EXP * HDIM, D), (HEADS * HDIM // 2) ** -0.5, 0.75, ((1, 4),))
    mlp_gain = jnp.clip(1.0 + 0.15 * jax.random.normal(streams_of[7], (D,), jnp.float32), 0.25, 1.75)
    mlp_router = scatter_about(streams_of[8], (D, EXPERTS), D ** -0.5, 0.09375)
    w_up = scatter_about(streams_of[9], (EXPERTS, D, MLP_HID), D ** -0.5, 0.09375, ((0, 16),))
    w_down = scatter_about(streams_of[10], (EXPERTS, MLP_HID, D), MLP_HID ** -0.5, 0.375, ((0, 16),))
    return dict(tokens=tokens, att_ids=att_ids, mlp_ids=mlp_ids, att_gain=att_gain, att_in=att_in, att_router=att_router, att_out=att_out, mlp_gain=mlp_gain, mlp_router=mlp_router, w_up=w_up, w_down=w_down)


epsilon = 1e-05

def rms_norm(values_in, gain_vector):
    floats = values_in.astype(jnp.float32)
    return floats * lax.rsqrt(lax.optimization_barrier(jnp.mean(floats * floats, axis=-1, keepdims=True)) + epsilon) * gain_vector

def reference(tokens, att_ids, mlp_ids, att_gain, att_in, att_router, att_out, mlp_gain, mlp_router, w_up, w_down):
    normed = rms_norm(tokens, att_gain).astype(jnp.bfloat16)
    proj = jnp.dot(normed, att_in, preferred_element_type=jnp.float32)
    head_width = HEADS * HDIM
    query = proj[:, :head_width].astype(jnp.bfloat16).reshape(TOKENS, HEADS, HDIM)
    keys = proj[:, head_width:2 * head_width].astype(jnp.bfloat16).reshape(TOKENS, HEADS, HDIM)
    value_all = proj[:, 2 * head_width:].reshape(TOKENS, HEADS, ATT_EXP, HDIM)
    att_logit = jnp.dot(normed, att_router, preferred_element_type=jnp.float32).reshape(TOKENS, HEADS, ATT_EXP)
    chosen = lax.optimization_barrier(jnp.sum((att_ids[..., None] == jnp.arange(ATT_EXP)[None, None, None, :]).astype(jnp.float32), axis=2))
    att_weight = jax.nn.sigmoid(att_logit) * chosen
    values = lax.optimization_barrier(jnp.sum(att_weight[..., None] * value_all, axis=2)).astype(jnp.bfloat16)
    scores = jnp.einsum('thd,shd->hts', query.astype(jnp.float32), keys.astype(jnp.float32), precision=lax.Precision.HIGHEST) * HDIM ** (-0.5)
    position = jnp.arange(TOKENS)
    causal = position[None, :] <= position[:, None]
    scores = jnp.where(causal[None], scores, -1e+30)
    probabilities = jax.nn.softmax(scores, axis=-1)
    attended = jnp.einsum('hts,shd->thd', probabilities, values.astype(jnp.float32), precision=lax.Precision.HIGHEST)
    head_normed = attended * lax.rsqrt(lax.optimization_barrier(jnp.mean(attended * attended, axis=-1, keepdims=True)) + epsilon)
    mixed = (head_normed[:, :, None, :] * att_weight[..., None]).reshape(TOKENS, HEADS * ATT_EXP * HDIM)
    mixed = mixed.astype(jnp.bfloat16)
    hidden_state = tokens.astype(jnp.float32) + jnp.dot(mixed, att_out, preferred_element_type=jnp.float32)
    mlp_in = rms_norm(hidden_state, mlp_gain).astype(jnp.bfloat16)
    logits = jnp.dot(mlp_in, mlp_router, preferred_element_type=jnp.float32)
    picked = (mlp_ids[..., None] == jnp.arange(EXPERTS)[None, None, :]).astype(jnp.float32)
    gates = jax.nn.sigmoid(lax.optimization_barrier(jnp.sum(picked * logits[:, None, :], axis=-1)))
    flat_ids = mlp_ids.reshape(-1)
    flat_gates = gates.reshape(-1)
    assignments = TOKENS * MLP_TOP
    slot_count = N_OUTER * N_INNER * CAP

    def one_expert(expert, accumulated):
        positions = jnp.nonzero(flat_ids == expert, size=slot_count, fill_value=assignments)[0].astype(jnp.int32)
        valid = (positions < assignments).astype(jnp.float32)
        clipped = jnp.minimum(positions, assignments - 1).astype(jnp.int32)
        token_index = (clipped // MLP_TOP).astype(jnp.int32)
        inputs = mlp_in[token_index]
        hidden = jnp.maximum(jnp.dot(inputs, w_up[expert], preferred_element_type=jnp.float32), 0.0)
        hidden = hidden.astype(jnp.bfloat16)
        result = jnp.dot(hidden, w_down[expert], preferred_element_type=jnp.float32).astype(jnp.bfloat16)
        weighted = (flat_gates[clipped] * valid)[:, None] * result.astype(jnp.float32)
        return accumulated.at[token_index].add(weighted)
    mlp_out = lax.fori_loop(0, EXPERTS, one_expert, jnp.zeros((TOKENS, D), jnp.float32))
    return (hidden_state + mlp_out).astype(jnp.bfloat16)
```

```python
import jax
import jax.numpy as jnp
import numpy as np
from jax import lax
from jax.sharding import PartitionSpec as P

D = 4096
HEADS = 2
HDIM = 64
ATT_EXP = 4
MLP_TOP = 8


epsilon = 1e-05


def rms_norm(values_in, gain_vector):
    floats = values_in.astype(jnp.float32)
    return (
        floats
        * lax.rsqrt(jnp.mean(floats * floats, axis=-1, keepdims=True) + epsilon)
        * gain_vector
    )


def moe(mlp_in, hidden_state, mlp_ids, mlp_router, w_up, w_down):
    rows, width = mlp_in.shape
    outer_count = lax.axis_size("outer")
    depth = lax.axis_size("inner")
    lanes = outer_count // 2
    local_experts = w_up.shape[0]
    outer = lax.axis_index("outer")
    z = lax.axis_index("inner")
    core = outer % 2
    x = outer // 2

    def place(xi, ci, zi):
        return (2 * xi + ci) * depth + zi

    def along_z(value, moves):
        pairs = [
            (place(xi, ci, a), place(xi, ci, b))
            for xi in range(lanes)
            for ci in range(2)
            for a, b in moves
        ]
        return lax.ppermute(value, ("outer", "inner"), pairs)

    def along_x(value, step, valid):
        pairs = [
            (place(xi, ci, zi), place((xi + step) % lanes, ci, zi))
            for xi in range(lanes)
            for ci in range(2)
            for zi in valid
        ]
        return lax.ppermute(value, ("outer", "inner"), pairs)

    def by_z(table):
        return jnp.asarray(np.asarray(table, np.int32))[z]

    sibling = [(o, o ^ 1) for o in range(outer_count)]
    up_own, up_other = w_up, lax.ppermute(w_up, "outer", sibling)
    down_own, down_other = w_down, lax.ppermute(w_down, "outer", sibling)
    ids = lax.all_gather(mlp_ids, ("outer", "inner"), axis=0, tiled=False)
    first_own = (outer * depth + z) * local_experts
    first_other = ((outer ^ 1) * depth + z) * local_experts
    experts = jnp.concatenate(
        [first_own + jnp.arange(local_experts), first_other + jnp.arange(local_experts)]
    )
    picked = jnp.sum(
        (ids[:, :, :, None] == experts[None, None, None, :]).astype(jnp.float32), axis=2
    )
    router = jnp.concatenate(
        [
            lax.dynamic_slice_in_dim(mlp_router, first_own, local_experts, 1),
            lax.dynamic_slice_in_dim(mlp_router, first_other, local_experts, 1),
        ],
        axis=1,
    )

    every = list(range(depth))
    left, right = {0: mlp_in}, {0: mlp_in}
    merged = {}
    units = {("own", 0): (mlp_in, every)}
    for s in range(1, depth):
        to_left = [(a, a - 1) for a in range(1, depth - s + 1)]
        to_right = [(a, a + 1) for a in range(s - 1, depth - 1)]
        if 2 * (s - 1) >= depth:
            merged[s] = along_z(merged[s - 1], to_left + to_right)
            units[("both", s)] = (merged[s], [a for a in every if a >= s or a < depth - s])
            continue
        left[s] = along_z(left[s - 1], to_right)
        right[s] = along_z(right[s - 1], to_left)
        if 2 * s >= depth:
            merged[s] = jnp.where(z >= s, left[s], right[s])
            units[("both", s)] = (merged[s], [a for a in every if a >= s or a < depth - s])
        else:
            units[("left", s)] = (left[s], [a for a in every if a >= s])
            units[("right", s)] = (right[s], [a for a in every if a < depth - s])

    def collect(found):
        blocks = [(found[("own", 0)], every)]
        for s in range(1, depth):
            if 2 * s < depth:
                near = jnp.where(z < s, found[("right", s)], found[("left", s)])
                blocks.append((near, [a + s if a < s else a - s for a in every]))
        for s in range(1, depth):
            if 2 * s == depth:
                blocks.append((found[("both", s)], [(a + s) % depth for a in every]))
        for s in reversed(range(1, depth)):
            if 2 * s < depth:
                far = jnp.where(
                    (z >= s) & (z < depth - s), found[("right", s)], found[("both", depth - s)]
                )
                blocks.append(
                    (
                        far,
                        [
                            a + depth - s if a < s else (a + s if a < depth - s else a - depth + s)
                            for a in every
                        ],
                    )
                )
        return blocks

    steps = [{name: unit[0] for name, unit in units.items()}]
    for step in range(1, lanes):
        steps.append({name: along_x(unit[0], step, unit[1]) for name, unit in units.items()})
    gathered = [collect(found) for found in steps]

    def hidden_of(block, step, table):
        owner = (2 * ((x - step) % lanes) + core) * depth + by_z(table)
        logits = jnp.dot(block, router, preferred_element_type=jnp.float32)
        gates = jax.nn.sigmoid(logits) * lax.dynamic_index_in_dim(picked, owner, 0, False)
        parts = []
        for e in range(2 * local_experts):
            weights = up_own[e] if e < local_experts else up_other[e - local_experts]
            part = jnp.dot(block, weights, preferred_element_type=jnp.float32)
            parts.append((jnp.maximum(part, 0.0) * gates[:, e : e + 1]).astype(jnp.bfloat16))
        return jnp.concatenate(parts, axis=1)

    hidden = []
    tables = [table for _, table in gathered[0]]
    for j in range(depth):
        hidden.append(
            jnp.stack([hidden_of(gathered[step][j][0], step, tables[j]) for step in range(lanes)])
        )
    hidden = jnp.stack(hidden)

    order = [sorted(every, key=lambda d: (-abs(d - a), d)) for a in every]
    unit_of = [[[t[a] for t in tables].index(d) for d in order[a]] for a in every]
    place_of = [[order[a].index(d) for d in every] for a in every]
    half = local_experts * w_down.shape[1]
    down = jnp.concatenate(
        [down_own.reshape(half, width), down_other.reshape(half, width)], axis=0
    )
    summed = []
    for k in range(depth):
        mine = lax.dynamic_index_in_dim(hidden, by_z([unit_of[a][k] for a in every]), 0, False)
        arrived = [
            along_x(
                jnp.dot(mine[step], down, preferred_element_type=jnp.float32).astype(jnp.bfloat16),
                -step,
                every,
            )
            for step in range(1, lanes)
        ]
        total = jnp.dot(mine[0], down, preferred_element_type=jnp.float32)
        for value in arrived:
            total = total + value.astype(jnp.float32)
        summed.append(total.astype(jnp.bfloat16))

    def choose(table):
        value = summed[table[0]]
        for a in every[1:]:
            if table[a] != table[a - 1]:
                value = jnp.where(z >= a, summed[table[a]], value)
        return value

    up_sum = down_sum = None
    for s in range(1, depth):
        senders = [a for a in every if a <= s - 1 and a + 1 < depth]
        table = [place_of[a][depth - s + a] if a in senders else None for a in every]
        known = [t for t in table if t is not None]
        table = [t if t is not None else known[-1] for t in table]
        value = choose(table)
        if up_sum is not None:
            value = (value.astype(jnp.float32) + up_sum.astype(jnp.float32)).astype(jnp.bfloat16)
        next_up = along_z(value, [(a, a + 1) for a in senders])
        senders = [a for a in every if depth - 1 - a <= s - 1 and a >= 1]
        table = [place_of[a][a + s - depth] if a in senders else None for a in every]
        known = [t for t in table if t is not None]
        table = [t if t is not None else known[0] for t in table]
        value = choose(table)
        if down_sum is not None:
            value = (value.astype(jnp.float32) + down_sum.astype(jnp.float32)).astype(jnp.bfloat16)
        next_down = along_z(value, [(a, a - 1) for a in senders])
        up_sum, down_sum = next_up, next_down
    result = hidden_state + summed[depth - 1].astype(jnp.float32)
    if up_sum is not None:
        result = result + up_sum.astype(jnp.float32) + down_sum.astype(jnp.float32)
    return result.astype(jnp.bfloat16)


def on_device(
    tokens,
    att_ids,
    mlp_ids,
    att_gain,
    att_in,
    att_router,
    att_out,
    mlp_gain,
    mlp_router,
    w_up,
    w_down,
):
    row_count = tokens.shape[0]
    head_width = HEADS * HDIM
    normed = rms_norm(tokens, att_gain).astype(jnp.bfloat16)
    proj = jnp.dot(
        normed,
        lax.all_gather(att_in, "inner", axis=0, tiled=True),
        preferred_element_type=jnp.float32,
    )
    att_logit = jnp.dot(
        normed,
        lax.all_gather(att_router, "inner", axis=0, tiled=True),
        preferred_element_type=jnp.float32,
    )
    query = proj[:, :head_width].astype(jnp.bfloat16).reshape(row_count, HEADS, HDIM)
    keys = proj[:, head_width : 2 * head_width].astype(jnp.bfloat16)
    value_all = proj[:, 2 * head_width :].reshape(row_count, HEADS, ATT_EXP, HDIM)
    chosen = jnp.sum(
        (att_ids[..., None] == jnp.arange(ATT_EXP)[None, None, None, :]).astype(jnp.float32), axis=2
    )
    att_weight = jax.nn.sigmoid(att_logit.reshape(row_count, HEADS, ATT_EXP)) * chosen
    values = (
        jnp.sum(att_weight[..., None] * value_all, axis=2)
        .astype(jnp.bfloat16)
        .reshape(row_count, head_width)
    )
    first_row = lax.axis_index(("outer", "inner")) * row_count
    query_position = first_row + jnp.arange(row_count)
    score_factor = HDIM ** (-0.5)
    start_state = (
        jnp.full((row_count, HEADS), -1e30, jnp.float32),
        jnp.zeros((row_count, HEADS), jnp.float32),
        jnp.zeros((row_count, HEADS, HDIM), jnp.float32),
    )
    block_keys = (
        lax.all_gather(keys, "inner", axis=0, tiled=True),
        lax.all_gather(values, "inner", axis=0, tiled=True),
    )
    key_piece = lax.all_gather(block_keys[0], "outer", axis=0, tiled=True)
    value_piece = lax.all_gather(block_keys[1], "outer", axis=0, tiled=True)
    piece_rows = key_piece.shape[0]

    def update(current):
        running_max, running_sum, accumulated = current
        key_heads = key_piece.reshape(piece_rows, HEADS, HDIM)
        value_heads = value_piece.reshape(piece_rows, HEADS, HDIM).astype(jnp.float32)
        scores = (
            jnp.einsum("thd,shd->ths", query, key_heads, preferred_element_type=jnp.float32)
            * score_factor
        )
        key_position = jnp.arange(piece_rows)
        visible = key_position[None, None, :] <= query_position[:, None, None]
        scores = jnp.where(visible, scores, -1e30)
        new_max = jnp.maximum(running_max, jnp.max(scores, axis=-1))
        weights = jnp.where(visible, jnp.exp(scores - new_max[..., None]), 0.0)
        new_sum = jnp.sum(weights, axis=-1)
        new_accum = jnp.einsum(
            "ths,shd->thd", weights, value_heads, precision=lax.Precision.HIGHEST
        )
        return (new_max, new_sum, new_accum)

    def keep_state(current):
        return current

    final_state = lax.cond(
        jnp.int32(0) <= first_row + row_count - 1, update, keep_state, start_state
    )
    attended = final_state[2] / final_state[1][..., None]
    head_normed = attended * lax.rsqrt(
        jnp.mean(attended * attended, axis=-1, keepdims=True) + epsilon
    )
    mixed = (head_normed[:, :, None, :] * att_weight[..., None]).reshape(
        row_count, HEADS * ATT_EXP * HDIM
    )
    mixed = mixed.astype(jnp.bfloat16)
    att_result = jnp.dot(
        mixed,
        lax.all_gather(att_out, "inner", axis=1, tiled=True),
        preferred_element_type=jnp.float32,
    )
    hidden_state = tokens.astype(jnp.float32) + att_result
    mlp_in = rms_norm(hidden_state, mlp_gain).astype(jnp.bfloat16)
    return moe(mlp_in, hidden_state, mlp_ids, mlp_router, w_up, w_down)


def solution(mesh):
    in_specs = (
        P(("seq", "outer", "inner"), None),
        P(("seq", "outer", "inner"), None, None),
        P(("seq", "outer", "inner"), None),
        P(),
        P("inner", None),
        P("inner", None),
        P(None, "inner"),
        P(),
        P(),
        P(("outer", "inner"), None, None),
        P(("outer", "inner"), None, None),
    )
    out_specs = P(("seq", "outer", "inner"), None)
    return jax.shard_map(
        on_device, mesh=mesh, in_specs=in_specs, out_specs=out_specs, check_vma=False
    )
```

```python
import jax
import jax.numpy as jnp
import numpy as np
from jax import lax
from jax.sharding import PartitionSpec as P

HEADS = 2
HDIM = 64
ATT_EXP = 4

epsilon = 1e-05


def rms_norm(values_in, gain_vector):
    floats = values_in.astype(jnp.float32)
    return (
        floats
        * lax.rsqrt(jnp.mean(floats * floats, axis=-1, keepdims=True) + epsilon)
        * gain_vector
    )


class Grid:
    def __init__(self):
        self.outer_count = lax.axis_size("outer")
        self.depth = lax.axis_size("inner")
        self.lanes = self.outer_count // 2
        self.twins = lax.axis_size("seq") // 2 * 2 == lax.axis_size("seq")
        self.outer = lax.axis_index("outer")
        self.z = lax.axis_index("inner")
        self.core = self.outer % 2
        self.x = self.outer // 2
        self.every = list(range(self.depth))

    def place(self, x, core, z):
        return (2 * x + core) * self.depth + z

    def permute(self, value, pairs):
        return lax.ppermute(value, ("outer", "inner"), pairs)

    def along_z(self, value, moves):
        return self.permute(
            value,
            [
                (self.place(x, core, a), self.place(x, core, b))
                for x in range(self.lanes)
                for core in range(2)
                for a, b in moves
            ],
        )

    def turn_z(self, value, step):
        return self.along_z(value, [(a, (a + step) % self.depth) for a in self.every])

    def along_x(self, value, step, valid):
        return self.permute(
            value,
            [
                (self.place(x, core, z), self.place((x + step) % self.lanes, core, z))
                for x in range(self.lanes)
                for core in range(2)
                for z in valid
            ],
        )

    def pair_x(self, value):
        return self.permute(
            value,
            [
                (self.place(x, core, z), self.place(x ^ 1, core, z))
                for x in range(self.lanes)
                for core in range(2)
                for z in self.every
            ],
        )

    def sibling(self, value):
        return lax.ppermute(value, "outer", [(o, o ^ 1) for o in range(self.outer_count)])

    def twin(self, value):
        return lax.ppermute(value, "seq", [(s, s ^ 1) for s in range(lax.axis_size("seq"))])

    def by_z(self, table):
        return jnp.asarray(np.asarray(table, np.int32))[self.z]

    def line(self, value):
        depth, every = self.depth, self.every
        left, right, both = {0: value}, {0: value}, {}
        units = {("own", 0): (value, every)}
        for s in range(1, depth):
            to_left = [(a, a - 1) for a in range(1, depth - s + 1)]
            to_right = [(a, a + 1) for a in range(s - 1, depth - 1)]
            outside = [a for a in every if a >= s or a < depth - s]
            if 2 * (s - 1) >= depth:
                both[s] = self.along_z(both[s - 1], to_left + to_right)
                units[("both", s)] = (both[s], outside)
                continue
            left[s] = self.along_z(left[s - 1], to_right)
            right[s] = self.along_z(right[s - 1], to_left)
            if 2 * s >= depth:
                both[s] = jnp.where(self.z >= s, left[s], right[s])
                units[("both", s)] = (both[s], outside)
            else:
                units[("left", s)] = (left[s], [a for a in every if a >= s])
                units[("right", s)] = (right[s], [a for a in every if a < depth - s])
        return units

    def collect(self, found):
        depth, every, z = self.depth, self.every, self.z
        blocks = [(found[("own", 0)], every)]
        for s in range(1, depth):
            if 2 * s < depth:
                near = jnp.where(z < s, found[("right", s)], found[("left", s)])
                blocks.append((near, [a + s if a < s else a - s for a in every]))
        for s in range(1, depth):
            if 2 * s == depth:
                blocks.append((found[("both", s)], [(a + s) % depth for a in every]))
        for s in reversed(range(1, depth)):
            if 2 * s < depth:
                inside = (z >= s) & (z < depth - s)
                far = jnp.where(inside, found[("right", s)], found[("both", depth - s)])
                table = [
                    a + depth - s if a < s else (a + s if a < depth - s else a - depth + s)
                    for a in every
                ]
                blocks.append((far, table))
        return blocks


def attention(grid, tokens, att_ids, att_gain, att_in, att_router, att_out):
    rows, width = tokens.shape
    depth = grid.depth
    z, x, core = grid.z, grid.x, grid.core
    head = x % HEADS
    head_width = HEADS * HDIM
    slots = ATT_EXP * HDIM
    shard = att_in.shape[0]

    normed = rms_norm(tokens, att_gain).astype(jnp.bfloat16)
    normed_pair = grid.pair_x(normed)
    ids = att_ids.reshape(rows, -1).T
    ids_pair = grid.pair_x(ids)

    def columns(h):
        return jnp.concatenate(
            [
                att_in[:, h * HDIM : (h + 1) * HDIM],
                att_in[:, head_width + h * HDIM : head_width + (h + 1) * HDIM],
                att_in[:, 2 * head_width + h * slots : 2 * head_width + (h + 1) * slots],
            ],
            axis=1,
        )

    own_weights = jnp.where(head == 0, columns(0), columns(1))
    piece = lax.dynamic_slice_in_dim(own_weights, core * (shard // 2), shard // 2, 0)
    units = grid.line(piece)
    blocks = grid.collect({name: unit[0] for name, unit in units.items()})
    whole = [(own_weights, blocks[0][1])]
    for value, table in blocks[1:]:
        other = grid.sibling(value)
        first = jnp.where(core == 0, value, other)
        second = jnp.where(core == 0, other, value)
        whole.append((jnp.concatenate([first, second], axis=0), table))
    router_own = att_router.T
    router_parts = [router_own] + [grid.turn_z(router_own, s) for s in range(1, depth)]
    router = jnp.stack(router_parts)[(z - jnp.arange(depth)) % depth]
    router = router.transpose(1, 0, 2).reshape(-1, width)

    def project(source, named):
        total = None
        for weights, table in whole:
            part = lax.dynamic_slice_in_dim(source, grid.by_z(table) * shard, shard, 1)
            product = jnp.dot(part, weights, preferred_element_type=jnp.float32)
            total = product if total is None else total + product
        logit = lax.dot_general(
            source, router, (((1,), (1,)), ((), ())), preferred_element_type=jnp.float32
        )
        chosen = jnp.sum(
            (
                named.reshape(HEADS, -1, 1, rows) == jnp.arange(ATT_EXP)[None, None, :, None]
            ).astype(jnp.float32),
            axis=1,
        )
        weight = jax.nn.sigmoid(logit) * chosen.reshape(HEADS * ATT_EXP, rows).T
        mine = jnp.where(head == 0, weight[:, :ATT_EXP], weight[:, ATT_EXP:])
        query = total[:, :HDIM].astype(jnp.bfloat16)
        keys = total[:, HDIM : 2 * HDIM].astype(jnp.bfloat16)
        values = sum(
            mine[:, e : e + 1] * total[:, (2 + e) * HDIM : (3 + e) * HDIM] for e in range(ATT_EXP)
        ).astype(jnp.bfloat16)
        return query, jnp.concatenate([keys, values], axis=1), weight

    query_own, pair_own, weight = project(normed, ids)
    query_other, pair_other, _ = project(normed_pair, ids_pair)
    query = jnp.concatenate([query_own, query_other], axis=0)
    known = jnp.concatenate([pair_own, pair_other], axis=0)

    groups = grid.lanes // HEADS
    known = jnp.stack([known] + [grid.along_x(known, HEADS * g, grid.every) for g in range(1, groups)])
    known = jnp.stack([known] + [grid.turn_z(known, s) for s in range(1, depth)])
    known = jnp.stack([known, grid.sibling(known)]).reshape(-1, 2 * HDIM)
    span = known.shape[0]
    index = jnp.arange(span)
    row = index % rows
    index = index // rows
    lane = x ^ (index % 2)
    index = index // 2
    lane = (lane - HEADS * (index % groups)) % grid.lanes
    index = index // groups
    from_z = (z - index % depth) % depth
    from_core = core ^ (index // depth)
    key_position = grid.place(lane, from_core, from_z) * rows + row
    own_row = jnp.arange(2 * rows)
    query_position = grid.place(x ^ (own_row // rows), core, z) * rows + own_row % rows
    scores = lax.dot_general(
        query, known[:, :HDIM], (((1,), (1,)), ((), ())), preferred_element_type=jnp.float32
    ) * HDIM ** (-0.5)
    visible = key_position[None, :] <= query_position[:, None]
    scores = jnp.where(visible, scores, -1e30)
    weights = jnp.exp(scores - jnp.max(scores, axis=-1, keepdims=True))
    attended = jnp.dot(
        weights, known[:, HDIM:].astype(jnp.float32), precision=lax.Precision.HIGHEST
    ) / jnp.sum(weights, axis=-1, keepdims=True)
    head_normed = attended * lax.rsqrt(
        jnp.mean(attended * attended, axis=-1, keepdims=True) + epsilon
    )
    returned = grid.pair_x(head_normed[rows:])
    by_head = [
        jnp.where(head == 0, head_normed[:rows], returned),
        jnp.where(head == 0, returned, head_normed[:rows]),
    ]

    twin = lax.axis_index("seq") % 2 if grid.twins else 0
    share = 4 if grid.twins else 2
    quarter = att_out.shape[0] // share
    first = 2 * twin + core
    piece = lax.dynamic_slice_in_dim(att_out, first * quarter, quarter, 0)
    late = [unit[0] for name, unit in units.items() if name[1] == max(1, depth - 2)]
    piece = lax.optimization_barrier(tuple([piece] + late))[0]
    out_units = grid.line(piece)
    out_blocks = grid.collect({name: unit[0] for name, unit in out_units.items()})
    gathered = []
    for value, table in out_blocks:
        parts = [value]
        if grid.twins:
            parts.append(grid.twin(value))
        parts = parts + [grid.sibling(part) for part in parts]
        gathered.append(jnp.concatenate(parts, axis=0))
    gathered = jnp.stack(gathered)
    position = [[table[a] for _, table in out_blocks].index(b) for b in grid.every for a in grid.every]
    position = np.asarray(position, np.int32).reshape(depth, depth)
    tiles = [by_head[h] * weight[:, h * ATT_EXP + e][:, None] for h in range(HEADS) for e in range(ATT_EXP)]
    mixed = jnp.concatenate(tiles, axis=1).astype(jnp.bfloat16)
    turns = [0, 2, 1, 3] if grid.twins else [0, 1]
    mixed = jnp.concatenate(
        [lax.dynamic_slice_in_dim(mixed, (first ^ t) * quarter, quarter, 1) for t in turns], axis=1
    )
    result = jnp.concatenate(
        [
            jnp.dot(
                mixed,
                lax.dynamic_index_in_dim(gathered, grid.by_z(position[b]), 0, False),
                preferred_element_type=jnp.float32,
            )
            for b in grid.every
        ],
        axis=1,
    )
    return tokens.astype(jnp.float32) + result


def moe(grid, mlp_in, hidden_state, mlp_ids, mlp_router, w_up, w_down):
    rows, width = mlp_in.shape
    depth, lanes, every = grid.depth, grid.lanes, grid.every
    z, x, outer = grid.z, grid.x, grid.outer
    local_experts = w_up.shape[0]
    along_x, along_z, by_z = grid.along_x, grid.along_z, grid.by_z

    up_own, up_other = w_up, grid.sibling(w_up)
    down_own, down_other = w_down, grid.sibling(w_down)
    first_own = (outer * depth + z) * local_experts
    first_other = ((outer ^ 1) * depth + z) * local_experts
    experts = jnp.concatenate(
        [first_own + jnp.arange(local_experts), first_other + jnp.arange(local_experts)]
    )
    ids = mlp_ids.T
    ids = jnp.stack([ids] + [grid.turn_z(ids, s) for s in range(1, depth)])
    ids = jnp.stack([ids] + [along_x(ids, step, every) for step in range(1, lanes)])
    picked = jnp.sum(
        (ids[:, :, :, None, :] == experts[None, None, None, :, None]).astype(jnp.float32), axis=2
    )
    router = jnp.concatenate(
        [
            lax.dynamic_slice_in_dim(mlp_router, first_own, local_experts, 1),
            lax.dynamic_slice_in_dim(mlp_router, first_other, local_experts, 1),
        ],
        axis=1,
    )

    units = grid.line(mlp_in)
    steps = [{name: unit[0] for name, unit in units.items()}]
    for step in range(1, lanes):
        steps.append({name: along_x(unit[0], step, unit[1]) for name, unit in units.items()})
    gathered = [grid.collect(found) for found in steps]

    def hidden_of(block, step, table):
        turn = (z - by_z(table)) % depth
        logits = jnp.dot(block, router, preferred_element_type=jnp.float32)
        gates = jax.nn.sigmoid(logits) * lax.dynamic_index_in_dim(picked[step], turn, 0, False).T
        parts = []
        for e in range(2 * local_experts):
            weights = up_own[e] if e < local_experts else up_other[e - local_experts]
            part = jnp.dot(block, weights, preferred_element_type=jnp.float32)
            parts.append((jnp.maximum(part, 0.0) * gates[:, e : e + 1]).astype(jnp.bfloat16))
        return jnp.concatenate(parts, axis=1)

    hidden = []
    tables = [table for _, table in gathered[0]]
    for j in range(depth):
        hidden.append(
            jnp.stack([hidden_of(gathered[step][j][0], step, tables[j]) for step in range(lanes)])
        )
    hidden = jnp.stack(hidden)

    order = [sorted(every, key=lambda d: (-abs(d - a), d)) for a in every]
    unit_of = [[[t[a] for t in tables].index(d) for d in order[a]] for a in every]
    place_of = [[order[a].index(d) for d in every] for a in every]
    half = local_experts * w_down.shape[1]
    down = jnp.concatenate(
        [down_own.reshape(half, width), down_other.reshape(half, width)], axis=0
    )
    summed = []
    for k in range(depth):
        mine = lax.dynamic_index_in_dim(hidden, by_z([unit_of[a][k] for a in every]), 0, False)
        arrived = [
            along_x(
                jnp.dot(mine[step], down, preferred_element_type=jnp.float32).astype(jnp.bfloat16),
                -step,
                every,
            )
            for step in range(1, lanes)
        ]
        total = jnp.dot(mine[0], down, preferred_element_type=jnp.float32)
        for value in arrived:
            total = total + value.astype(jnp.float32)
        summed.append(total.astype(jnp.bfloat16))

    def choose(table):
        value = summed[table[0]]
        for a in every[1:]:
            if table[a] != table[a - 1]:
                value = jnp.where(z >= a, summed[table[a]], value)
        return value

    up_sum = down_sum = None
    for s in range(1, depth):
        senders = [a for a in every if a <= s - 1 and a + 1 < depth]
        table = [place_of[a][depth - s + a] if a in senders else None for a in every]
        known = [t for t in table if t is not None]
        table = [t if t is not None else known[-1] for t in table]
        value = choose(table)
        if up_sum is not None:
            value = (value.astype(jnp.float32) + up_sum.astype(jnp.float32)).astype(jnp.bfloat16)
        next_up = along_z(value, [(a, a + 1) for a in senders])
        senders = [a for a in every if depth - 1 - a <= s - 1 and a >= 1]
        table = [place_of[a][a + s - depth] if a in senders else None for a in every]
        known = [t for t in table if t is not None]
        table = [t if t is not None else known[0] for t in table]
        value = choose(table)
        if down_sum is not None:
            value = (value.astype(jnp.float32) + down_sum.astype(jnp.float32)).astype(jnp.bfloat16)
        next_down = along_z(value, [(a, a - 1) for a in senders])
        up_sum, down_sum = next_up, next_down
    result = hidden_state + summed[depth - 1].astype(jnp.float32)
    if up_sum is not None:
        result = result + up_sum.astype(jnp.float32) + down_sum.astype(jnp.float32)
    return result.astype(jnp.bfloat16)


def on_device(
    tokens,
    att_ids,
    mlp_ids,
    att_gain,
    att_in,
    att_router,
    att_out,
    mlp_gain,
    mlp_router,
    w_up,
    w_down,
):
    grid = Grid()
    hidden_state = attention(grid, tokens, att_ids, att_gain, att_in, att_router, att_out)
    mlp_in = rms_norm(hidden_state, mlp_gain).astype(jnp.bfloat16)
    return moe(grid, mlp_in, hidden_state, mlp_ids, mlp_router, w_up, w_down)


def solution(mesh):
    in_specs = (
        P(("seq", "outer", "inner"), None),
        P(("seq", "outer", "inner"), None, None),
        P(("seq", "outer", "inner"), None),
        P(),
        P("inner", None),
        P("inner", None),
        P(None, "inner"),
        P(),
        P(),
        P(("outer", "inner"), None, None),
        P(("outer", "inner"), None, None),
    )
    out_specs = P(("seq", "outer", "inner"), None)
    return jax.shard_map(
        on_device, mesh=mesh, in_specs=in_specs, out_specs=out_specs, check_vma=False
    )
```

```python
import jax
import jax.numpy as jnp
import numpy as np
from jax import lax
from jax.experimental import pallas as pl
from jax.experimental.pallas import tpu as pltpu
from jax.sharding import PartitionSpec as P

HEADS = 2
HDIM = 64
ATT_EXP = 4

epsilon = 1e-05


def rms_norm(values_in, gain_vector):
    floats = values_in.astype(jnp.float32)
    return (
        floats
        * lax.rsqrt(jnp.mean(floats * floats, axis=-1, keepdims=True) + epsilon)
        * gain_vector
    )


class Grid:
    def __init__(self):
        self.outer_count = lax.axis_size("outer")
        self.depth = lax.axis_size("inner")
        self.lanes = self.outer_count // 2
        self.twins = lax.axis_size("seq") // 2 * 2 == lax.axis_size("seq")
        self.outer = lax.axis_index("outer")
        self.z = lax.axis_index("inner")
        self.core = self.outer % 2
        self.x = self.outer // 2
        self.every = list(range(self.depth))
        self.share = 4 if self.twins else 2
        self.turns = [0, 2, 1, 3] if self.twins else [0, 1]
        twin = lax.axis_index("seq") % 2 if self.twins else 0
        self.quarter = 2 * twin + self.core

    def place(self, x, core, z):
        return (2 * x + core) * self.depth + z

    def permute(self, value, pairs):
        return lax.ppermute(value, ("outer", "inner"), pairs)

    def along_z(self, value, moves):
        return self.permute(
            value,
            [
                (self.place(x, core, a), self.place(x, core, b))
                for x in range(self.lanes)
                for core in range(2)
                for a, b in moves
            ],
        )

    def turn_z(self, value, step):
        return self.along_z(value, [(a, (a + step) % self.depth) for a in self.every])

    def source(self, x, step):
        return ((x ^ (step % HEADS)) - step // HEADS * HEADS) % self.lanes

    def along_x(self, value, step, valid=None, back=False):
        pairs = [
            (self.place(self.source(x, step), core, z), self.place(x, core, z))
            for x in range(self.lanes)
            for core in range(2)
            for z in (self.every if valid is None else valid)
        ]
        return self.permute(value, [(b, a) for a, b in pairs] if back else pairs)

    def sibling(self, value):
        return lax.ppermute(value, "outer", [(o, o ^ 1) for o in range(self.outer_count)])

    def twin(self, value):
        return lax.ppermute(value, "seq", [(s, s ^ 1) for s in range(lax.axis_size("seq"))])

    def by_z(self, table):
        return jnp.asarray(np.asarray(table, np.int32))[self.z]

    def line(self, value):
        depth, every = self.depth, self.every
        left, right, both = {0: value}, {0: value}, {}
        units = {("own", 0): (value, every)}
        for s in range(1, depth):
            to_left = [(a, a - 1) for a in range(1, depth - s + 1)]
            to_right = [(a, a + 1) for a in range(s - 1, depth - 1)]
            outside = [a for a in every if a >= s or a < depth - s]
            if 2 * (s - 1) >= depth:
                both[s] = self.along_z(both[s - 1], to_left + to_right)
                units[("both", s)] = (both[s], outside)
                continue
            left[s] = self.along_z(left[s - 1], to_right)
            right[s] = self.along_z(right[s - 1], to_left)
            if 2 * s >= depth:
                both[s] = jnp.where(self.z >= s, left[s], right[s])
                units[("both", s)] = (both[s], outside)
            else:
                units[("left", s)] = (left[s], [a for a in every if a >= s])
                units[("right", s)] = (right[s], [a for a in every if a < depth - s])
        return units

    def collect(self, found):
        depth, every, z = self.depth, self.every, self.z
        blocks = [(found[("own", 0)], every)]
        for s in range(1, depth):
            if 2 * s < depth:
                near = jnp.where(z < s, found[("right", s)], found[("left", s)])
                blocks.append((near, [a + s if a < s else a - s for a in every]))
        for s in range(1, depth):
            if 2 * s == depth:
                blocks.append((found[("both", s)], [(a + s) % depth for a in every]))
        for s in reversed(range(1, depth)):
            if 2 * s < depth:
                inside = (z >= s) & (z < depth - s)
                far = jnp.where(inside, found[("right", s)], found[("both", depth - s)])
                table = [
                    a + depth - s if a < s else (a + s if a < depth - s else a - depth + s)
                    for a in every
                ]
                blocks.append((far, table))
        return blocks


MIB = 1 << 20


def whole(shape, memory_space=pltpu.VMEM):
    return pl.BlockSpec(memory_space=memory_space)


def call(body, outs, *operands, flops=0, scratch=()):
    moved = sum(a.size * a.dtype.itemsize for a in operands)
    moved += sum(int(np.prod(o.shape)) * o.dtype.itemsize for o in outs)
    return pl.pallas_call(
        body,
        out_shape=outs,
        in_specs=[pl.BlockSpec(memory_space=pltpu.SMEM)]
        + [pl.BlockSpec(memory_space=pltpu.VMEM)] * (len(operands) - 1),
        out_specs=[pl.BlockSpec(memory_space=pltpu.VMEM)] * len(outs),
        scratch_shapes=list(scratch),
        compiler_params=pltpu.CompilerParams(vmem_limit_bytes=48 * MIB),
        cost_estimate=pl.CostEstimate(flops=flops, bytes_accessed=moved, transcendentals=0),
    )(*operands)


def pick_columns(grid, att_in):
    rows = att_in.shape[0]
    part = rows // grid.share
    head_width, slots = HEADS * HDIM, ATT_EXP * HDIM
    width = 2 * HDIM + slots

    def body(at, source, own, piece):
        for h in range(HEADS):

            @pl.when(at[0] == h)
            def _():
                own[:, : 2 * HDIM] = jnp.concatenate(
                    [
                        source[:, h * HDIM : (h + 1) * HDIM],
                        source[:, head_width + h * HDIM : head_width + (h + 1) * HDIM],
                    ],
                    axis=1,
                )
                own[:, 2 * HDIM :] = source[
                    :, 2 * head_width + h * slots : 2 * head_width + (h + 1) * slots
                ]

        piece[...] = own[pl.ds(pl.multiple_of(at[1] * part, part), part), :]

    at = jnp.stack([grid.x % HEADS, grid.quarter]).astype(jnp.int32)
    return call(
        body,
        [
            jax.ShapeDtypeStruct((rows, width), att_in.dtype),
            jax.ShapeDtypeStruct((part, width), att_in.dtype),
        ],
        at,
        att_in,
    )


def project(grid, normed, normed_pair, chosen, own, arrived, routers):
    rows, width = normed.shape
    shard = own.shape[0]
    part = shard // grid.share
    columns = own.shape[1]
    depth = grid.depth
    count = len(arrived[0]) if arrived else 0

    def body(at, mine, other, named, held, *refs):
        router_refs = refs[:depth]
        refs = refs[depth:]
        pieces, (query, known, weight, total) = refs[: count * (depth - 1)], refs[count * (depth - 1) :]

        def rows_of(start, size):
            span = pl.ds(pl.multiple_of(start, 128), size)
            return jnp.concatenate([mine[:, span], other[:, span]], axis=0)

        logit = jnp.zeros((2 * rows, HEADS * ATT_EXP), jnp.float32)
        for s in range(depth):
            block = lax.rem(at[0] + (depth - s), depth) * shard
            logit = logit + lax.dot_general(
                rows_of(block, shard),
                router_refs[s][:, :shard],
                (((1,), (1,)), ((), ())),
                preferred_element_type=jnp.float32,
            )
            if s == 0:
                total[...] = jnp.dot(
                    rows_of(block, shard), held[...], preferred_element_type=jnp.float32
                )
                continue
            turn = 0
            for piece in pieces[(s - 1) * count : s * count]:
                for first in range(0, piece.shape[0], part):
                    start = block + lax.bitwise_xor(at[1], grid.turns[turn]) * part
                    turn += 1
                    total[...] += jnp.dot(
                        rows_of(start, part),
                        piece[first : first + part, :],
                        preferred_element_type=jnp.float32,
                    )
        chance = jax.nn.sigmoid(logit) * named[...]
        weight[...] = chance[:rows]
        picked = jnp.where(at[2] == 0, chance[:, :ATT_EXP], chance[:, ATT_EXP:])
        query[...] = total[:, :HDIM].astype(jnp.bfloat16)
        mixed = jnp.zeros((2 * rows, HDIM), jnp.float32)
        for e in range(ATT_EXP):
            mixed = mixed + picked[:, e : e + 1] * total[:, (2 + e) * HDIM : (3 + e) * HDIM]
        known[...] = jnp.concatenate(
            [total[:, HDIM : 2 * HDIM].astype(jnp.bfloat16), mixed.astype(jnp.bfloat16)], axis=1
        )

    at = jnp.stack([grid.z, grid.quarter, grid.x % HEADS]).astype(jnp.int32)
    return call(
        body,
        [
            jax.ShapeDtypeStruct((2 * rows, HDIM), jnp.bfloat16),
            jax.ShapeDtypeStruct((2 * rows, 2 * HDIM), jnp.bfloat16),
            jax.ShapeDtypeStruct((rows, HEADS * ATT_EXP), jnp.float32),
        ],
        at,
        normed,
        normed_pair,
        chosen,
        own,
        *routers,
        *[piece for group in arrived for piece in group],
        flops=4 * rows * width * columns,
        scratch=[pltpu.VMEM((2 * rows, columns), jnp.float32)],
    )


def finish(grid, tokens, by_head, weight, att_out, arrived, gain):
    rows, width = tokens.shape
    inner, shard = att_out.shape
    part = inner // grid.share
    depth = grid.depth

    def body(at, source, first, second, weights, scale, held, *refs):
        pieces, (hidden, normed, mixed) = refs[:-3], refs[-3:]
        heads = [first, second]
        for h in range(HEADS):
            for e in range(ATT_EXP):
                tile = h * ATT_EXP + e
                mixed[:, tile * HDIM : (tile + 1) * HDIM] = (
                    heads[h][...] * weights[:, tile : tile + 1]
                ).astype(jnp.bfloat16)
        squares = jnp.zeros((rows, 1), jnp.float32)
        for s in range(depth):
            block = lax.rem(at[0] + (depth - s), depth) * shard
            span = pl.ds(pl.multiple_of(block, 128), shard)
            if s == 0:
                value = jnp.dot(mixed[...], held[...], preferred_element_type=jnp.float32)
            else:
                value = jnp.zeros((rows, shard), jnp.float32)
                turn = 0
                for piece in pieces:
                    for k in range(piece.shape[0]):
                        start = lax.bitwise_xor(at[1], grid.turns[turn]) * part
                        turn += 1
                        value = value + jnp.dot(
                            mixed[:, pl.ds(pl.multiple_of(start, 128), part)],
                            piece[k, s - 1],
                            preferred_element_type=jnp.float32,
                        )
            value = value + source[:, span].astype(jnp.float32)
            hidden[:, span] = value
            squares = squares + jnp.sum(value * value, axis=1, keepdims=True)
        factor = lax.rsqrt(squares / width + epsilon)
        normed[...] = (hidden[...] * factor * scale[...]).astype(jnp.bfloat16)

    at = jnp.stack([grid.z, grid.quarter]).astype(jnp.int32)
    return call(
        body,
        [
            jax.ShapeDtypeStruct((rows, width), jnp.float32),
            jax.ShapeDtypeStruct((rows, width), jnp.bfloat16),
        ],
        at,
        tokens,
        by_head[0],
        by_head[1],
        weight,
        gain.reshape(1, width),
        att_out,
        *arrived,
        flops=2 * rows * width * inner,
        scratch=[pltpu.VMEM((rows, inner), jnp.bfloat16)],
    )


def expert_hidden(held, j, depth, blocks, masks, router, up_own, up_other):
    rows, width = blocks[0].shape
    lanes = len(blocks)
    local, _, units = up_own.shape
    steps = 4
    chunk = width // steps
    tall = lanes * rows
    total = 2 * local * units

    def body(*refs):
        if held is not None:
            refs = refs[1:]
        sources, (mask, route, own, other, out, sum_own, sum_other, gates) = refs[:lanes], refs[lanes:]
        e, k = pl.program_id(0), pl.program_id(1)

        @pl.when((e == 0) & (k == 0))
        def _():
            for i in range(lanes):
                logit = lax.dot_general(
                    sources[i][...],
                    route[...],
                    (((1,), (1,)), ((), ())),
                    preferred_element_type=jnp.float32,
                )
                here = pl.ds(i * rows, rows)
                gates[here, :] = jax.nn.sigmoid(logit) * mask[here, :]

        span = pl.ds(pl.multiple_of(k * chunk, chunk), chunk)
        value = jnp.concatenate([source[:, span] for source in sources], axis=0)
        for weights, acc in ((own, sum_own), (other, sum_other)):
            product = jnp.dot(value, weights[0], preferred_element_type=jnp.float32)

            @pl.when(k == 0)
            def _():
                acc[...] = product

            @pl.when(k > 0)
            def _():
                acc[...] += product

        @pl.when(k == steps - 1)
        def _():
            for first, acc in ((0, sum_own), (local, sum_other)):
                for i in range(local):

                    @pl.when(e == i)
                    def _():
                        column = first + i
                        scaled = jnp.maximum(acc[...], 0.0) * gates[:, column : column + 1]
                        out[0, :, column * units : (column + 1) * units] = scaled.astype(jnp.bfloat16)

    fixed = lambda e, k: (0, 0)
    weight_spec = pl.BlockSpec((1, chunk, units), lambda e, k: (e, k, 0))
    operands = list(blocks) + [masks, router, up_own, up_other]
    specs = [pl.BlockSpec((rows, width), fixed)] * lanes
    specs += [
        pl.BlockSpec(masks.shape, fixed),
        pl.BlockSpec(router.shape, fixed),
        weight_spec,
        weight_spec,
    ]
    aliases = {}
    if held is not None:
        operands = [held] + operands
        specs = [pl.BlockSpec(memory_space=pl.ANY)] + specs
        aliases = {0: 0}
    return pl.pallas_call(
        body,
        grid=(local, steps),
        out_shape=jax.ShapeDtypeStruct((depth, tall, total), jnp.bfloat16),
        in_specs=specs,
        out_specs=pl.BlockSpec((1, tall, total), lambda e, k: (j, 0, 0)),
        scratch_shapes=[
            pltpu.VMEM((tall, units), jnp.float32),
            pltpu.VMEM((tall, units), jnp.float32),
            pltpu.VMEM(masks.shape, jnp.float32),
        ],
        input_output_aliases=aliases,
        compiler_params=pltpu.CompilerParams(vmem_limit_bytes=32 * MIB),
        cost_estimate=pl.CostEstimate(
            flops=2 * tall * width * total,
            bytes_accessed=2 * width * (total + tall),
            transcendentals=0,
        ),
    )(*operands)


def expert_result(hidden, unit, lanes, down_own, down_other):
    depth, tall, total = hidden.shape
    rows = tall // lanes
    half, width = down_own.shape
    chunk = 512

    def body(at, source, own, other, *outs):
        value = jnp.dot(source[0, :, :half], own[...], preferred_element_type=jnp.float32)
        value = value + jnp.dot(source[0, :, half:], other[...], preferred_element_type=jnp.float32)
        for i in range(lanes):
            outs[i][...] = value[i * rows : (i + 1) * rows].astype(jnp.bfloat16)

    weight_spec = pl.BlockSpec((half, chunk), lambda n, at: (0, n))
    return pl.pallas_call(
        body,
        grid_spec=pltpu.PrefetchScalarGridSpec(
            num_scalar_prefetch=1,
            grid=(width // chunk,),
            in_specs=[
                pl.BlockSpec((1, tall, total), lambda n, at: (at[0], 0, 0)),
                weight_spec,
                weight_spec,
            ],
            out_specs=[pl.BlockSpec((rows, chunk), lambda n, at: (0, n))] * lanes,
        ),
        out_shape=[jax.ShapeDtypeStruct((rows, width), jnp.bfloat16)] * lanes,
        compiler_params=pltpu.CompilerParams(vmem_limit_bytes=32 * MIB),
        cost_estimate=pl.CostEstimate(
            flops=2 * tall * width * total,
            bytes_accessed=2 * width * (total + tall),
            transcendentals=0,
        ),
    )(unit.reshape(1), hidden, down_own, down_other)


def attention(grid, tokens, att_ids, mlp_ids, att_gain, att_in, att_router, att_out, mlp_gain):
    rows, width = tokens.shape
    depth, lanes = grid.depth, grid.lanes
    z, x, core = grid.z, grid.x, grid.core
    head = x % HEADS

    own, piece = pick_columns(grid, att_in)
    pieces = [grid.turn_z(piece, s) for s in range(1, depth)]
    normed = rms_norm(tokens, att_gain).astype(jnp.bfloat16)
    normed_pair = grid.along_x(normed, 1)

    named = jnp.concatenate([mlp_ids.T, att_ids.reshape(rows, -1).T], axis=0).astype(jnp.bfloat16)
    named = lax.optimization_barrier((named, normed))[0]
    named = [named] + [grid.along_x(named, step) for step in range(1, lanes)]
    top = mlp_ids.shape[1]
    small = jnp.concatenate([att_router.T] + [ids[:top] for ids in named], axis=1)
    small = [small] + [grid.turn_z(small, s) for s in range(1, depth)]

    def chosen_of(ids):
        hits = ids[top:].reshape(HEADS, -1, 1, rows) == jnp.arange(ATT_EXP)[None, None, :, None]
        return jnp.sum(hits.astype(jnp.float32), axis=1).reshape(HEADS * ATT_EXP, rows).T

    chosen = jnp.concatenate([chosen_of(named[0]), chosen_of(named[1])], axis=0)

    arrived = []
    for value in pieces:
        parts = [value]
        if grid.twins:
            twin = grid.twin(value)
            parts = [value, twin]
            arrived.append(parts + [grid.sibling(jnp.concatenate(parts, axis=0))])
        else:
            arrived.append(parts + [grid.sibling(value)])
    query, known, weight = project(grid, normed, normed_pair, chosen, own, arrived, small)

    part = att_out.shape[0] // grid.share
    piece = lax.dynamic_slice_in_dim(att_out, grid.quarter * part, part, 0)
    piece = lax.optimization_barrier(tuple([piece] + pieces))[0]
    outs = [jnp.stack([grid.turn_z(piece, s) for s in range(1, depth)])[None]]
    if grid.twins:
        outs.append(grid.twin(outs[0]))
    outs.append(grid.sibling(jnp.concatenate(outs, axis=0)))

    groups = lanes // HEADS
    known = jnp.stack([known] + [grid.along_x(known, HEADS * g) for g in range(1, groups)])
    known = jnp.stack([known] + [grid.turn_z(known, s) for s in range(1, depth)])
    known = jnp.stack([known, grid.sibling(known)]).reshape(-1, 2 * HDIM)
    span = known.shape[0]
    index = jnp.arange(span)
    row = index % rows
    index = index // rows
    lane = x ^ (index % 2)
    index = index // 2
    lane = (lane - HEADS * (index % groups)) % lanes
    index = index // groups
    from_z = (z - index % depth) % depth
    from_core = core ^ (index // depth)
    key_position = grid.place(lane, from_core, from_z) * rows + row
    own_row = jnp.arange(2 * rows)
    query_position = grid.place(x ^ (own_row // rows), core, z) * rows + own_row % rows
    scores = lax.dot_general(
        query, known[:, :HDIM], (((1,), (1,)), ((), ())), preferred_element_type=jnp.float32
    ) * HDIM ** (-0.5)
    visible = key_position[None, :] <= query_position[:, None]
    scores = jnp.where(visible, scores, -1e30)
    weights = jnp.exp(scores - jnp.max(scores, axis=-1, keepdims=True))
    attended = jnp.dot(
        weights, known[:, HDIM:].astype(jnp.float32), precision=lax.Precision.HIGHEST
    ) / jnp.sum(weights, axis=-1, keepdims=True)
    head_normed = attended * lax.rsqrt(
        jnp.mean(attended * attended, axis=-1, keepdims=True) + epsilon
    )
    returned = grid.along_x(head_normed[rows:], 1)
    by_head = [
        jnp.where(head == 0, head_normed[:rows], returned),
        jnp.where(head == 0, returned, head_normed[:rows]),
    ]
    hidden_state, mlp_in = finish(grid, tokens, by_head, weight, att_out, outs, mlp_gain)
    shard = att_router.shape[0]
    ids = [
        [small[s][:, shard + step * rows : shard + (step + 1) * rows] for s in range(depth)]
        for step in range(lanes)
    ]
    return hidden_state, mlp_in, jnp.stack([jnp.stack(of) for of in ids])


def moe(grid, mlp_in, hidden_state, ids, mlp_router, up_pair, down_pair):
    rows, width = mlp_in.shape
    depth, lanes, every = grid.depth, grid.lanes, grid.every
    z, x, outer = grid.z, grid.x, grid.outer
    up_own, up_other = up_pair
    local_experts = up_own.shape[0]
    along_x, along_z, by_z = grid.along_x, grid.along_z, grid.by_z
    half = local_experts * up_own.shape[2]
    down_own, down_other = [value.reshape(half, width) for value in down_pair]
    first_own = (outer * depth + z) * local_experts
    first_other = ((outer ^ 1) * depth + z) * local_experts
    experts = jnp.concatenate(
        [first_own + jnp.arange(local_experts), first_other + jnp.arange(local_experts)]
    )
    picked = jnp.sum(
        (ids[:, :, :, None, :] == experts.astype(ids.dtype)[None, None, None, :, None]).astype(
            jnp.float32
        ),
        axis=2,
    )
    router = jnp.concatenate(
        [
            lax.dynamic_slice_in_dim(mlp_router, first_own, local_experts, 1),
            lax.dynamic_slice_in_dim(mlp_router, first_other, local_experts, 1),
        ],
        axis=1,
    ).T

    units = grid.line(mlp_in)
    steps = [{name: unit[0] for name, unit in units.items()}]
    for step in range(1, lanes):
        steps.append({name: along_x(unit[0], step, unit[1]) for name, unit in units.items()})
    gathered = [grid.collect(found) for found in steps]

    hidden = None
    tables = [table for _, table in gathered[0]]
    for j in range(depth):
        turn = (z - by_z(tables[j])) % depth
        masks = lax.dynamic_index_in_dim(picked, turn, 1, False)
        masks = masks.transpose(0, 2, 1).reshape(lanes * rows, -1)
        blocks = [gathered[step][j][0] for step in range(lanes)]
        hidden = expert_hidden(hidden, j, depth, blocks, masks, router, up_own, up_other)

    order = [sorted(every, key=lambda d: (-abs(d - a), d)) for a in every]
    unit_of = [[[t[a] for t in tables].index(d) for d in order[a]] for a in every]
    place_of = [[order[a].index(d) for d in every] for a in every]
    summed = []
    for k in range(depth):
        unit = by_z([unit_of[a][k] for a in every])
        sums = expert_result(hidden, unit, lanes, down_own, down_other)
        total = sums[0].astype(jnp.float32)
        for step in range(1, lanes):
            total = total + along_x(sums[step], step, back=True).astype(jnp.float32)
        summed.append(total.astype(jnp.bfloat16))

    def choose(table):
        value = summed[table[0]]
        for a in every[1:]:
            if table[a] != table[a - 1]:
                value = jnp.where(z >= a, summed[table[a]], value)
        return value

    def outgoing(s, rising, received):
        senders = [a for a in every if (a if rising else depth - 1 - a) <= s - 1]
        table = [
            place_of[a][depth - s + a if rising else a + s - depth] if a in senders else None
            for a in every
        ]
        known = [t for t in table if t is not None]
        table = [t if t is not None else known[-1 if rising else 0] for t in table]
        value = choose(table)
        if received is not None:
            value = (value.astype(jnp.float32) + received.astype(jnp.float32)).astype(jnp.bfloat16)
        return value, [(a, a + 1 if rising else a - 1) for a in senders]

    up_sum = down_sum = None
    for s in range(1, depth):
        rising, up_moves = outgoing(s, True, up_sum)
        falling, down_moves = outgoing(s, False, down_sum)
        if 2 * s < depth - 1:
            up_sum = down_sum = along_z(jnp.where(z < s, rising, falling), up_moves + down_moves)
        else:
            up_sum = along_z(rising, up_moves)
            down_sum = along_z(falling, down_moves)
    result = hidden_state + summed[depth - 1].astype(jnp.float32)
    if up_sum is not None:
        result = result + up_sum.astype(jnp.float32) + down_sum.astype(jnp.float32)
    return result.astype(jnp.bfloat16)


def on_device(
    tokens,
    att_ids,
    mlp_ids,
    att_gain,
    att_in,
    att_router,
    att_out,
    mlp_gain,
    mlp_router,
    w_up,
    w_down,
):
    grid = Grid()
    hidden_state, mlp_in, ids = attention(
        grid, tokens, att_ids, mlp_ids, att_gain, att_in, att_router, att_out, mlp_gain
    )
    up_pair = (w_up, grid.sibling(w_up))
    down_pair = (w_down, grid.sibling(w_down))
    return moe(grid, mlp_in, hidden_state, ids, mlp_router, up_pair, down_pair)


def solution(mesh):
    in_specs = (
        P(("seq", "outer", "inner"), None),
        P(("seq", "outer", "inner"), None, None),
        P(("seq", "outer", "inner"), None),
        P(),
        P("inner", None),
        P("inner", None),
        P(None, "inner"),
        P(),
        P(),
        P(("outer", "inner"), None, None),
        P(("outer", "inner"), None, None),
    )
    out_specs = P(("seq", "outer", "inner"), None)
    return jax.shard_map(
        on_device, mesh=mesh, in_specs=in_specs, out_specs=out_specs, check_vma=False
    )
```
